256 devices in a mesh: sess: 8 (over x_lo, y), exp: 32 (over x_hi, z, core).
Axes of the slice: x: 4 (x_hi: 2, x_lo: 2; x = x_hi * 2 + x_lo), y: 4, z: 8, core: 2. Of those that a mesh axis runs over, the one named last changes fastest.
Arguments:
- tokens: bfloat16 [8192, 2048], P(('sess', 'exp')), may hold values from -6 to 6
- thinker_gain: float32 [2048], replicated, may hold values from 0.25 to 1.75
- thinker_ids: int32 [8192, 8], P(('sess', 'exp')), may hold values from 0 to 31, all different within a row; in each aligned block of 32 rows (0 to 31, 32 to 63, ...) at most 16 rows name the same one
- thinker_gates: float32 [8192, 8], P(('sess', 'exp')), may hold values from 0.05 to 0.25
- w_gate: bfloat16 [32, 2048, 768], P('exp'), may hold values from -0.125 to 0.125
- w_up: bfloat16 [32, 2048, 768], P('exp'), may hold values from -0.125 to 0.125
- w_down: bfloat16 [32, 768, 2048], P('exp'), may hold values from -0.21875 to 0.21875
- talker_in: bfloat16 [8192, 1024], P(('sess', 'exp')), may hold values from -6 to 6
- talker_gain: float32 [1024], replicated, may hold values from 0.25 to 1.75
- talker_ids: int32 [8192, 2], P(('sess', 'exp')), may hold values from 0 to 7, all different within a row; in each aligned block of 32 rows (0 to 31, 32 to 63, ...) at most 16 rows name the same one
- talker_gates: float32 [8192, 2], P(('sess', 'exp')), may hold values from 0.2 to 0.6
- t_gate: bfloat16 [8, 1024, 384], P('sess'), may hold values from -0.1875 to 0.1875
- t_up: bfloat16 [8, 1024, 384], P('sess'), may hold values from -0.1875 to 0.1875
- t_down: bfloat16 [8, 384, 1024], P('sess'), may hold values from -0.3125 to 0.3125
- conv_state: float32 [8192, 3, 1024], P(('sess', 'exp')), may hold values from -6 to 6
- conv_kernel: float32 [4, 1024], replicated, may hold values from -3 to 3
- conv_gain: float32 [1024], replicated, may hold values from 0.25 to 1.75
Outputs:
- thought: bfloat16 [8192, 2048], P(('sess', 'exp'))
- spoken: bfloat16 [8192, 1024], P(('sess', 'exp'))
- audio_frame: bfloat16 [8192, 1024], P(('sess', 'exp'))
- new_state: float32 [8192, 3, 1024], P(('sess', 'exp'))
The draws below stay inside these ranges and needn't reach their ends.
Inputs may be any that keep to these rules, and one draw needn't show every extreme that they name: `thinker_ids`: each row names 8 different experts; within the 32 rows of one device no expert is named by more than 16 rows. `talker_ids`: each row names 2 different experts; within the 32 rows of one device no expert is named by more than 16 rows.
All inputs are finite; a program needn't handle non-finite values.
Results may differ from the reference program's by a relative error of at most 0.0055.
Values may be sent and summed in bfloat16 or wider, within the bound.
No kernel may reach another device: no remote copies, remote signals or barrier semaphores. Data moves between devices by JAX's collectives and lax.ppermute only.
A program may use at most 64 MiB of HBM per device.

```python
import math
import jax
import jax.numpy as jnp
import numpy as np
from jax import lax

D = 2048
FF = 768
TOP = 8
DT = 1024
FT = 384
TTOP = 2
KW = 4
SESS_DEV = 32
EXPERTS = 32
TEXP = 8
SESSIONS = 8192
CAP = 16
CAPT = 16


def shard_levels(own_key, shape, split, least, top_value):
    level, own = 1.0, jax.random.fold_in(own_key, 6)
    for dim, parts in split:
        steps = jnp.exp(jax.random.uniform(jax.random.fold_in(own, dim), (parts,), jnp.float32, least / len(split), top_value / len(split)))
        level = level * jnp.repeat(steps, shape[dim] // parts).reshape([-1 if axis == dim else 1 for axis in range(len(shape))])
    return level


def deal_out(key, own, number, rows, count, top, limit, slope):
    sequence = jax.random.permutation(key, count)
    heavy_load, ordinary = shares(count, rows * top, limit, slope, True), shares(count, rows * top, limit, slope, False)
    places = jnp.arange(count)

    def named(tallies, turn):
        used = int((tallies > 0).sum())
        fixed = max(1, used // 4)
        passed = fixed + (places - fixed + turn * (used - fixed)) % max(1, count - fixed)
        return jnp.zeros((count,), jnp.int32).at[sequence[jnp.where(places < fixed, places, passed)]].set(jnp.asarray(tallies, jnp.int32))

    tallies = jnp.where(number % 4 == 0, named(heavy_load, number // 4), named(ordinary, number - number // 4 - 1))
    mixed = jax.random.permutation(jax.random.fold_in(own, 3), count)
    donor, receiver = mixed[0:count // 2 * 2:2], mixed[1:count // 2 * 2:2]
    room = jnp.minimum(tallies[donor] - 1, limit - tallies[receiver]) // 2
    room = jnp.where((donor == sequence[0]) | (receiver == sequence[0]) | (tallies[receiver] == 0), 0, jnp.maximum(room, 0))
    passed = jax.random.randint(jax.random.fold_in(own, 4), (count // 2,), 0, 1 << 20) % (room + 1)
    tallies = tallies.at[donor].add(-passed).at[receiver].add(passed)
    items = jnp.searchsorted(jnp.cumsum(tallies), jnp.arange(rows * top), side="right").astype(jnp.int32)
    grid = items.reshape(top, rows).T
    grid = grid[jax.random.permutation(jax.random.fold_in(own, 1), rows)]
    turn = jax.random.randint(jax.random.fold_in(own, 2), (rows, 1), 0, top)
    return jnp.take_along_axis(grid, (jnp.arange(top)[None, :] + turn) % top, axis=1)


def shares(number_of, total, bound, slope, full):
    loads = [(1 << 20) // math.isqrt(grade ** slope) + 1 for grade in range(1, number_of + 1)]
    largest = bound if full else min(bound, max(-(-total // number_of), total * loads[0] // sum(loads)))
    least = 1 if total - largest >= number_of - 1 else 0
    holding, rest = [largest] + [least] * (number_of - 1), total - largest - least * (number_of - 1)
    while rest > 0:
        free = [i for i in range(1, number_of) if holding[i] < largest] or [i for i in range(1, number_of) if holding[i] < bound]
        whole, remaining = sum([loads[i] for i in free]), rest
        for i in free:
            addition = min(bound - holding[i], max(1, remaining * loads[i] // whole), rest)
            holding[i] = holding[i] + addition
            rest = rest - addition
    return np.array(holding)


def noise(rng, dims, scale, most, shards=(), held_as=jnp.bfloat16):
    array = jax.random.normal(rng, dims, jnp.float32) * scale
    if len(shards) > 0:
        array = shard_levels(rng, dims, shards, -0.22, 0.18) * array
    return jnp.clip(array, min=-most, max=most).astype(held_as)


def setup_inputs(seed: int = 0) -> dict:
    seeds = jax.random.split(jax.random.key(seed), 18)
    tokens = noise(seeds[0], (SESSIONS, D), 1.0, 6.0, ((0, 256),))
    thinker_gain = jnp.clip(1.0 + 0.15 * jax.random.normal(seeds[1], (D,), jnp.float32), 0.25, 1.75)
    thinker_ids_keys = jax.random.split(jax.random.fold_in(seeds[2], 1), SESSIONS // SESS_DEV)
    thinker_ids_turns = jax.random.permutation(jax.random.fold_in(seeds[2], 3), SESSIONS // SESS_DEV)
    thinker_ids = jax.vmap(lambda own, number: deal_out(jax.random.fold_in(seeds[2], 2), own, number, SESS_DEV, EXPERTS, TOP, CAP, 2))(thinker_ids_keys, thinker_ids_turns).reshape((SESSIONS, TOP))
    thinker_gates = jnp.clip(0.05 + 0.2 * jax.random.uniform(seeds[3], (SESSIONS, TOP), jnp.float32) ** shard_levels(seeds[3], (SESSIONS, TOP), ((0, 256),), -0.2, 0.2), 0.05, 0.25)
    w_gate = noise(seeds[4], (EXPERTS, D, FF), D ** -0.5, 0.125, ((0, 32),))
    w_up = noise(seeds[5], (EXPERTS, D, FF), D ** -0.5, 0.125, ((0, 32),))
    w_down = noise(seeds[6], (EXPERTS, FF, D), FF ** -0.5, 0.21875, ((0, 32),))
    talker_in = noise(seeds[7], (SESSIONS, DT), 1.0, 6.0, ((0, 256),))
    talker_gain = jnp.clip(1.0 + 0.15 * jax.random.normal(seeds[8], (DT,), jnp.float32), 0.25, 1.75)
    talker_ids_keys = jax.random.split(jax.random.fold_in(seeds[9], 1), SESSIONS // SESS_DEV)
    talker_ids_turns = jax.random.permutation(jax.random.fold_in(seeds[9], 3), SESSIONS // SESS_DEV)
    talker_ids = jax.vmap(lambda own, number: deal_out(jax.random.fold_in(seeds[9], 2), own, number, SESS_DEV, TEXP, TTOP, CAPT, 2))(talker_ids_keys, talker_ids_turns).reshape((SESSIONS, TTOP))
    talker_gates = jnp.clip(0.2 + 0.400000021 * jax.random.uniform(seeds[10], (SESSIONS, TTOP), jnp.float32) ** shard_levels(seeds[10], (SESSIONS, TTOP), ((0, 256),), -0.2, 0.2), 0.2, 0.6)
    t_gate = noise(seeds[11], (TEXP, DT, FT), DT ** -0.5, 0.1875, ((0, 8),))
    t_up = noise(seeds[12], (TEXP, DT, FT), DT ** -0.5, 0.1875, ((0, 8),))
    t_down = noise(seeds[13], (TEXP, FT, DT), FT ** -0.5, 0.3125, ((0, 8),))
    conv_state = noise(seeds[14], (SESSIONS, KW - 1, DT), 1.0, 6.0, ((0, 256),), jnp.float32)
    conv_kernel = noise(seeds[15], (KW, DT), 0.5, 3.0, (), jnp.float32)
    conv_gain = jnp.clip(1.0 + 0.15 * jax.random.normal(seeds[16], (DT,), jnp.float32), 0.25, 1.75)
    return dict(tokens=tokens, thinker_gain=thinker_gain, thinker_ids=thinker_ids, thinker_gates=thinker_gates, w_gate=w_gate, w_up=w_up, w_down=w_down, talker_in=talker_in, talker_gain=talker_gain, talker_ids=talker_ids, talker_gates=talker_gates, t_gate=t_gate, t_up=t_up, t_down=t_down, conv_state=conv_state, conv_kernel=conv_kernel, conv_gain=conv_gain)


def rms_scale(values, gain):
    wide = values.astype(jnp.float32)
    scale = lax.rsqrt(lax.optimization_barrier(jnp.mean(wide * wide, axis=-1, keepdims=True)) + 1e-06)
    return (wide * scale * gain).astype(jnp.bfloat16)

def bucket_slots(ids, count):
    onehot = (ids[:, :, None] == jnp.arange(count, dtype=jnp.int32)).astype(jnp.int32)
    used = lax.optimization_barrier(jnp.sum(onehot, axis=1, dtype=jnp.int32))
    before = jnp.cumsum(used, axis=0, dtype=jnp.int32) - used
    return lax.optimization_barrier(jnp.sum(onehot * before[:, None, :], axis=2, dtype=jnp.int32))

def expert_rows(rows, weight_gate, weight_up, weight_down):
    gate = jnp.dot(rows, weight_gate, preferred_element_type=jnp.float32)
    up = jnp.dot(rows, weight_up, preferred_element_type=jnp.float32)
    hidden = (jax.nn.silu(gate) * up).astype(jnp.bfloat16)
    return jnp.dot(hidden, weight_down, preferred_element_type=jnp.float32).astype(jnp.bfloat16)

def moe_layer(values, gain, ids, gates, weight_gate, weight_up, weight_down, count, capacity, blocks):
    sessions = values.shape[0]
    per_block = sessions // blocks
    normed = rms_scale(values, gain)
    slots = jax.vmap(lambda group: bucket_slots(group, count))(ids.reshape(blocks, per_block, -1))
    slots = slots.reshape(ids.shape)
    block_of = (jnp.arange(sessions, dtype=jnp.int32) // per_block)[:, None]
    places = block_of * capacity + slots
    rows_all = blocks * capacity

    def visit(expert, total):
        chosen = ids == expert
        has_any = jnp.any(chosen, axis=1)
        where_row = lax.optimization_barrier(jnp.sum(jnp.where(chosen, places, 0), axis=1, dtype=jnp.int32))
        weight = lax.optimization_barrier(jnp.sum(jnp.where(chosen, gates, 0.0), axis=1))
        target = jnp.where(has_any, where_row, rows_all).astype(jnp.int32)
        rows = jnp.zeros((rows_all, values.shape[1]), jnp.bfloat16).at[target].set(normed, mode='drop')
        result = expert_rows(rows, lax.dynamic_index_in_dim(weight_gate, expert, 0, keepdims=False), lax.dynamic_index_in_dim(weight_up, expert, 0, keepdims=False), lax.dynamic_index_in_dim(weight_down, expert, 0, keepdims=False))
        picked = jnp.take(result, where_row, axis=0)
        return total + weight[:, None] * picked.astype(jnp.float32)
    total = lax.fori_loop(0, count, visit, jnp.zeros(values.shape, jnp.float32))
    return (values.astype(jnp.float32) + total).astype(jnp.bfloat16)

def reference(tokens, thinker_gain, thinker_ids, thinker_gates, w_gate, w_up, w_down, talker_in, talker_gain, talker_ids, talker_gates, t_gate, t_up, t_down, conv_state, conv_kernel, conv_gain):
    blocks = SESSIONS // SESS_DEV
    thought = moe_layer(tokens, thinker_gain, thinker_ids, thinker_gates, w_gate, w_up, w_down, EXPERTS, CAP, blocks)
    spoken = moe_layer(talker_in, talker_gain, talker_ids, talker_gates, t_gate, t_up, t_down, TEXP, CAPT, blocks)
    window = jnp.concatenate([conv_state, spoken.astype(jnp.float32)[:, None, :]], axis=1)
    mixed = lax.optimization_barrier(jnp.sum(window * conv_kernel[None, :, :], axis=1))
    scale = lax.rsqrt(lax.optimization_barrier(jnp.mean(mixed * mixed, axis=-1, keepdims=True)) + 1e-06)
    audio_frame = (mixed * scale * conv_gain).astype(jnp.bfloat16)
    new_state = window[:, 1:, :]
    return (thought, spoken, audio_frame, new_state)
```

```python
import jax
import jax.numpy as jnp
from jax import lax
from jax.sharding import PartitionSpec as P


XH, ZN, CN = 2, 8, 2


def routes(move):
    pairs = []
    for x in range(XH):
        for z in range(ZN):
            for c in range(CN):
                a, b, d = move(x, z, c)
                pairs.append(((x * ZN + z) * CN + c, ((a % XH) * ZN + b % ZN) * CN + d % CN))
    return pairs


UP = routes(lambda x, z, c: (x, z + 1, c))
DOWN = routes(lambda x, z, c: (x, z - 1, c))
CORE = routes(lambda x, z, c: (x, z, c + 1))
CROSS = routes(lambda x, z, c: (x + 1, z, c))


def move(values, route):
    return lax.ppermute(values, "exp", route)


def rms_scale(values, gain):
    wide = values.astype(jnp.float32)
    scale = lax.rsqrt(jnp.mean(wide * wide, axis=-1, keepdims=True) + 1e-06)
    return (wide * scale * gain).astype(jnp.bfloat16)


def bucket_slots(ids, count):
    onehot = (ids[:, :, None] == jnp.arange(count, dtype=jnp.int32)).astype(jnp.int32)
    used = jnp.sum(onehot, axis=1, dtype=jnp.int32)
    before = jnp.cumsum(used, axis=0, dtype=jnp.int32) - used
    return jnp.sum(onehot * before[:, None, :], axis=2, dtype=jnp.int32)


def expert_rows(rows, weight_gate, weight_up, weight_down):
    gate = jnp.dot(rows, weight_gate, preferred_element_type=jnp.float32)
    up = jnp.dot(rows, weight_up, preferred_element_type=jnp.float32)
    hidden = (jax.nn.silu(gate) * up).astype(jnp.bfloat16)
    return jnp.dot(hidden, weight_down, preferred_element_type=jnp.float32).astype(jnp.bfloat16)


def fill_buckets(normed, places, count, capacity):
    grid = jnp.arange(count * capacity, dtype=jnp.int32)
    select = jnp.any(places[:, :, None] == grid, axis=1).astype(jnp.bfloat16)
    filled = jnp.einsum("tp,td->pd", select, normed, preferred_element_type=jnp.float32)
    return filled.astype(jnp.bfloat16).reshape(count, capacity, normed.shape[1])


def combine_back(values, returned, places, gates):
    flat = returned.reshape(-1, returned.shape[2])
    grid = jnp.arange(flat.shape[0], dtype=jnp.int32)
    picked = jnp.take(flat, places.reshape(-1), axis=0).reshape(
        places.shape[0], places.shape[1], -1
    )
    total = jnp.sum(gates[:, :, None] * picked.astype(jnp.float32), axis=1)
    return (values.astype(jnp.float32) + total).astype(jnp.bfloat16)


def thinker(tokens, gain, ids, gates, w_gate, w_up, w_down):
    n = tokens.shape[0]
    here = lax.axis_index("exp")
    my_x, my_z, my_c = here // (ZN * CN), (here // CN) % ZN, here % CN
    named = ids[:, :, None] == jnp.arange(XH * ZN * CN, dtype=jnp.int32)
    weights = jnp.sum(jnp.where(named, gates[:, :, None], 0.0), axis=1).T
    weights = lax.all_to_all(weights, "exp", split_axis=0, concat_axis=0, tiled=True)

    near, far = {0: tokens}, {0: move(tokens, CROSS)}
    for k in range(1, 4):
        near[-k] = move(near[1 - k], UP)
        near[k] = move(near[k - 1], DOWN)
        far[-k] = move(far[1 - k], UP)
        far[k] = move(far[k - 1], DOWN)
    near[4] = move(near[-3], UP)
    far[4] = move(far[3], DOWN)

    partial = {}
    for group in ((0,), (-1, 1), (-2, 2), (-3, 3), (4,)):
        mine = jnp.concatenate([part for o in group for part in (near[o], far[o])])
        other = move(mine, CORE)
        rows = jnp.concatenate([mine, other])
        source = jnp.stack(
            [
                ((my_x + x) % XH * ZN + (my_z + o) % ZN) * CN + (my_c + c) % CN
                for c in range(CN)
                for o in group
                for x in range(XH)
            ]
        )
        weight = jnp.take(weights, source, axis=0).reshape(-1, 1)
        out = expert_rows(rms_scale(rows, gain), w_gate, w_up, w_down)
        out = weight * out.astype(jnp.float32)
        half = mine.shape[0]
        summed = out[:half] + move(out[half:].astype(jnp.bfloat16), CORE).astype(jnp.float32)
        for i, o in enumerate(group):
            partial[o] = (summed[2 * i * n : (2 * i + 1) * n], summed[(2 * i + 1) * n : (2 * i + 2) * n])

    def chain(which, steps, route, sign):
        total = partial[sign * steps if steps < 4 else 4][which]
        for k in range(steps - 1, -1, -1):
            total = move(total.astype(jnp.bfloat16), route).astype(jnp.float32)
            if k > 0:
                total = total + partial[sign * k][which]
        return total

    far_total = chain(1, 3, UP, 1) + chain(1, 4, DOWN, -1) + partial[0][1]
    near_total = chain(0, 4, UP, 1) + chain(0, 3, DOWN, -1) + partial[0][0]
    back = move(far_total.astype(jnp.bfloat16), CROSS).astype(jnp.float32)
    return (tokens.astype(jnp.float32) + near_total + back).astype(jnp.bfloat16)


def shards(
    tokens,
    thinker_gain,
    thinker_ids,
    thinker_gates,
    w_gate,
    w_up,
    w_down,
    talker_in,
    talker_gain,
    talker_ids,
    talker_gates,
    t_gate,
    t_up,
    t_down,
    conv_state,
    conv_kernel,
    conv_gain,
):
    sess_dev = tokens.shape[0]
    owners = lax.axis_size("sess") * t_gate.shape[0]
    talk_capacity = min(sess_dev, 2 * sess_dev * talker_ids.shape[1] // owners)
    thought = thinker(tokens, thinker_gain, thinker_ids, thinker_gates, w_gate[0], w_up[0], w_down[0])
    normed = rms_scale(talker_in, talker_gain)
    places = talker_ids * talk_capacity + bucket_slots(talker_ids, owners)
    buckets = fill_buckets(normed, places, owners, talk_capacity)
    rows = lax.all_to_all(buckets, "sess", split_axis=0, concat_axis=0, tiled=True)
    sources = rows.shape[0]
    slots_here = rows.shape[1]
    flat = rows.reshape(sources * slots_here, rows.shape[2])
    result = expert_rows(flat, t_gate[0], t_up[0], t_down[0]).reshape(sources, slots_here, -1)
    returned = lax.all_to_all(result, "sess", split_axis=0, concat_axis=0, tiled=True)
    spoken = combine_back(talker_in, returned, places, talker_gates)
    window = jnp.concatenate([conv_state, spoken.astype(jnp.float32)[:, None, :]], axis=1)
    mixed = jnp.sum(window * conv_kernel[None, :, :], axis=1)
    scale = lax.rsqrt(jnp.mean(mixed * mixed, axis=-1, keepdims=True) + 1e-06)
    audio_frame = (mixed * scale * conv_gain).astype(jnp.bfloat16)
    new_state = window[:, 1:, :]
    return (thought, spoken, audio_frame, new_state)


def solution(mesh):
    rows = P(("sess", "exp"), None)
    rows3 = P(("sess", "exp"), None, None)
    placed = (
        rows,
        P(),
        rows,
        rows,
        P("exp", None, None),
        P("exp", None, None),
        P("exp", None, None),
        rows,
        P(),
        rows,
        rows,
        P("sess", None, None),
        P("sess", None, None),
        P("sess", None, None),
        rows3,
        P(),
        P(),
    )
    return jax.shard_map(
        shards,
        mesh=mesh,
        in_specs=placed,
        out_specs=(rows, rows, rows, rows3),
        check_vma=False,
    )
```

```python
import functools

import jax
import jax.numpy as jnp
from jax import lax
from jax.experimental import pallas as pl
from jax.experimental.pallas import tpu as pltpu
from jax.sharding import PartitionSpec as P


XH, ZN, CN = 2, 8, 2
LANES = 128
F32, BF16 = jnp.float32, jnp.bfloat16
VMEM = pl.BlockSpec(memory_space=pltpu.VMEM)
HBM = pl.BlockSpec(memory_space=pltpu.HBM)


def routes(move):
    pairs = []
    for x in range(XH):
        for z in range(ZN):
            for c in range(CN):
                a, b, d = move(x, z, c)
                pairs.append(((x * ZN + z) * CN + c, ((a % XH) * ZN + b % ZN) * CN + d % CN))
    return pairs


UP = routes(lambda x, z, c: (x, z + 1, c))
DOWN = routes(lambda x, z, c: (x, z - 1, c))
CORE = routes(lambda x, z, c: (x, z, c + 1))
CROSS = routes(lambda x, z, c: (x + 1, z, c))


XL, YN = 2, 4


def turns(dx, dy):
    return [(x * YN + y, (x + dx) % XL * YN + (y + dy) % YN) for x in range(XL) for y in range(YN)]


def move(values, route, name):
    with jax.named_scope(name):
        return lax.ppermute(values, "exp", route)


def turn(values, dx, dy, name):
    with jax.named_scope(name):
        return lax.ppermute(values, "sess", turns(dx, dy))


def on_chip(values):
    return pltpu.with_memory_space_constraint(values, pltpu.VMEM)


def call(kernel, out_shape, *args, scratch=(), limit=6, far_args=()):
    fetched = len(far_args)

    def body(*refs):
        sources, refs = refs[:fetched], refs[fetched:]
        if fetched:
            targets, semaphores, refs = refs[-fetched - 1 : -1], refs[-1], refs[: -fetched - 1]
            copies = [
                pltpu.make_async_copy(source, target, semaphores.at[i])
                for i, (source, target) in enumerate(zip(sources, targets))
            ]
            for copy in copies:
                copy.start()
            for copy in copies:
                copy.wait()
            refs = (*targets, *refs)
        kernel(*refs)

    extra = [pltpu.VMEM(arg.shape, arg.dtype) for arg in far_args]
    if fetched:
        extra.append(pltpu.SemaphoreType.DMA((fetched,)))
    return pl.pallas_call(
        body,
        out_shape=out_shape,
        in_specs=[HBM] * fetched + [VMEM] * len(args),
        out_specs=jax.tree.map(lambda _: VMEM, out_shape),
        scratch_shapes=[*scratch, *extra],
        compiler_params=pltpu.CompilerParams(vmem_limit_bytes=limit << 20),
    )(*far_args, *args)


def shape(rows, columns, dtype=BF16):
    return jax.ShapeDtypeStruct((rows, columns), dtype)


def chip(rows, columns, dtype=BF16):
    return pltpu.VMEM((rows, columns), dtype)


def normalize(values, gain):
    wide = values.astype(F32)
    scale = lax.rsqrt(jnp.mean(wide * wide, axis=-1, keepdims=True) + 1e-06)
    return (wide * scale * gain).astype(BF16)


def three_parts(values):
    high = values.astype(BF16)
    rest = values - high.astype(F32)
    middle = rest.astype(BF16)
    low = (rest - middle.astype(F32)).astype(BF16)
    return high, middle, low


def thinker_prepare(experts, tokens, gain, ids, gates, out):
    width = tokens.shape[1]
    out[:, :width] = normalize(tokens[...], gain[...])
    lane = lax.broadcasted_iota(jnp.int32, (LANES, tokens.shape[0]), 0)
    named = lane % experts
    weight = jnp.zeros(lane.shape, F32)
    for k in range(ids.shape[0]):
        weight += jnp.where(ids[k : k + 1, :] == named, gates[k : k + 1, :], 0.0)
    high, middle, low = (part.astype(F32) for part in three_parts(weight))
    piece = lane // experts
    tags = jnp.where(piece == 0, high, jnp.where(piece == 1, middle, jnp.where(piece == 2, low, 0.0)))
    out[:, width:] = tags.T.astype(BF16)


def thinker_experts(experts, count, fetch, *refs):
    rows, refs = refs[: 4 * count], refs[4 * count :]
    weights, refs = refs[:3], refs[3:]
    if fetch:
        sources, weights = weights, refs[2 * count + 1 : 2 * count + 4]
        semaphores, refs = refs[-1], refs[:-1]
    mine, other, packed, hidden = refs[: 2 * count], refs[2 * count], refs[-2], refs[-1]
    if fetch:
        copies = [pltpu.make_async_copy(sources[i], weights[i], semaphores.at[i]) for i in range(3)]
        for copy in copies:
            copy.start()
    w_gate, w_up, w_down = weights
    n, width = rows[0].shape[0], w_gate.shape[0]
    lane = lax.broadcasted_iota(jnp.int32, (n, LANES), 1)
    chosen = (lane % experts == lax.axis_index("exp")) & (lane < 3 * experts)
    scales = []
    for i, row in enumerate(rows):
        packed[i * n : (i + 1) * n, :] = row[:, :width]
        tags = row[:, width:].astype(F32)
        scales.append(jnp.sum(jnp.where(chosen, tags, 0.0), axis=1, keepdims=True))
    tile = 256
    if fetch:
        copies[0].wait()
        copies[1].wait()

    def raise_tile(j, carry):
        at = pl.ds(pl.multiple_of(j * tile, tile), tile)
        gate = jnp.dot(packed[...], w_gate[:, at], preferred_element_type=F32)
        up = jnp.dot(packed[...], w_up[:, at], preferred_element_type=F32)
        hidden[:, at] = (gate / (1.0 + jnp.exp(-gate)) * up).astype(BF16)
        return carry

    lax.fori_loop(0, w_gate.shape[1] // tile, raise_tile, 0)
    if fetch:
        copies[2].wait()

    def lower_tile(j, carry):
        at = pl.ds(pl.multiple_of(j * tile, tile), tile)
        result = jnp.dot(hidden[...], w_down[:, at], preferred_element_type=F32).astype(BF16)
        for i in range(4 * count):
            part = scales[i] * result[i * n : (i + 1) * n].astype(F32)
            if i < 2 * count:
                mine[i][:, at] = part
            else:
                other[(i - 2 * count) * n : (i - 2 * count + 1) * n, at] = part.astype(BF16)
        return carry

    lax.fori_loop(0, width // tile, lower_tile, 0)


def open_chain(at, mine, across, out):
    out[...] = (mine[...] + across[at : at + mine.shape[0], :].astype(F32)).astype(BF16)


def pass_on(ats, *refs):
    count = len(ats)
    for i, at in enumerate(ats):
        came, mine, across = refs[3 * i : 3 * i + 3]
        out = refs[3 * count + i]
        share = mine[...] + across[at : at + mine.shape[0], :].astype(F32)
        out[...] = (came[...].astype(F32) + share).astype(BF16)


def close_far(at, up, down, mine, across, out):
    share = mine[...] + across[at : at + mine.shape[0], :].astype(F32)
    out[...] = (up[...].astype(F32) + down[...].astype(F32) + share).astype(BF16)


def close_near(at, tokens, up, down, mine, across, back, out):
    share = mine[...] + across[at : at + mine.shape[0], :].astype(F32)
    total = up[...].astype(F32) + down[...].astype(F32) + share + back[...].astype(F32)
    out[...] = (tokens[...].astype(F32) + total).astype(BF16)


def thinker(tokens, gain, ids, gates, w_gate, w_up, w_down):
    n, width = tokens.shape
    experts = lax.axis_size("exp")
    with jax.named_scope("prep"):
        rows = call(
            functools.partial(thinker_prepare, experts),
            chip(n, width + LANES),
            far_args=(tokens, gain.reshape(1, -1), ids.T, gates.T),
        )
    near, far = {0: rows}, {0: on_chip(move(rows, CROSS, "x"))}
    for k in range(1, 4):
        near[-k] = on_chip(move(near[1 - k], UP, f"n{k}u"))
        near[k] = on_chip(move(near[k - 1], DOWN, f"n{k}d"))
        far[-k] = on_chip(move(far[1 - k], UP, f"f{k}u"))
        far[k] = on_chip(move(far[k - 1], DOWN, f"f{k}d"))
    near[4] = on_chip(move(near[-3], UP, "n4u"))
    far[4] = on_chip(move(far[3], DOWN, "f4d"))

    mine, across, place = {}, {}, {}
    weights = [w_gate, w_up, w_down]
    for turn_of, group in enumerate(((0, -1, 1), (-2, 2), (-3, 3), (4,))):
        own = [part for o in group for part in (near[o], far[o])]
        beside = [on_chip(move(part, CORE, f"c{turn_of}")) for part in own]
        count, fetch = len(group), turn_of == 0
        outs = [chip(n, width, F32)] * (2 * count) + [chip(2 * count * n, width)]
        scratch = [pltpu.VMEM((4 * count * n, width), BF16), pltpu.VMEM((4 * count * n, w_gate.shape[1]), BF16)]
        if fetch:
            outs += [pltpu.VMEM(w.shape, w.dtype) for w in weights]
            scratch.append(pltpu.SemaphoreType.DMA((3,)))
        with jax.named_scope(f"g{turn_of}"):
            parts = pl.pallas_call(
                functools.partial(thinker_experts, experts, count, fetch),
                out_shape=outs,
                in_specs=[VMEM] * (4 * count) + [HBM if fetch else VMEM] * 3,
                out_specs=[VMEM] * len(outs),
                scratch_shapes=scratch,
                compiler_params=pltpu.CompilerParams(vmem_limit_bytes=16 << 20),
            )(*own, *beside, *weights)
        if fetch:
            weights = [on_chip(w) for w in parts[-3:]]
        other = on_chip(move(parts[2 * count], CORE, f"r{turn_of}"))
        for i, o in enumerate(group):
            mine[o] = parts[2 * i : 2 * i + 2]
            across[o] = other
            place[o] = 2 * i * n

    def start(which, o):
        return call(
            functools.partial(open_chain, place[o] + which * n),
            chip(n, width),
            mine[o][which],
            across[o],
        )

    def step(which, came, offsets):
        args = []
        for value, o in zip(came, offsets):
            args += [on_chip(value), mine[o][which], across[o]]
        return call(
            functools.partial(pass_on, [place[o] + which * n for o in offsets]),
            [chip(n, width)] * len(offsets),
            *args,
        )

    def ring(which, up_first):
        long, short = (UP, DOWN) if up_first else (DOWN, UP)
        sign = 1 if up_first else -1
        name = "qf" if which else "qn"
        two = move(start(which, -sign * 3), short, name + "s1")
        one = move(start(which, 4), long, name + "l1")
        one_sum, two_sum = step(which, (one, two), (sign * 3, -sign * 2))
        one, two = move(one_sum, long, name + "l2"), move(two_sum, short, name + "s2")
        one_sum, two_sum = step(which, (one, two), (sign * 2, -sign * 1))
        one, two = move(one_sum, long, name + "l3"), move(two_sum, short, name + "s3")
        (one_sum,) = step(which, (one,), (sign * 1,))
        return on_chip(move(one_sum, long, name + "l4")), on_chip(two)

    far_one, far_two = ring(1, True)
    near_one, near_two = ring(0, False)
    back = call(
        functools.partial(close_far, place[0] + n),
        chip(n, width),
        far_one,
        far_two,
        mine[0][1],
        across[0],
    )
    back = on_chip(move(back, CROSS, "qx"))
    return call(
        functools.partial(close_near, place[0]),
        shape(n, width),
        near_one,
        near_two,
        mine[0][0],
        across[0],
        back,
        far_args=(tokens,),
    )


def talker_places(owners, capacity, ids):
    count, n = ids.shape
    here = lax.axis_index("sess")
    owner = lax.broadcasted_iota(jnp.int32, (owners, n), 0)
    used = jnp.zeros((owners, n), F32)
    for k in range(count):
        used += jnp.where(ids[k : k + 1, :] == owner, 1.0, 0.0)
    row = lax.broadcasted_iota(jnp.int32, (n, n), 0)
    column = lax.broadcasted_iota(jnp.int32, (n, n), 1)
    earlier = jnp.where(row < column, 1.0, 0.0).astype(BF16)
    before = jnp.dot(used.astype(BF16), earlier, preferred_element_type=F32)
    places = []
    for k in range(count):
        named = ids[k : k + 1, :]
        slot = jnp.sum(jnp.where(named == owner, before, 0.0), axis=0, keepdims=True)
        dx = (named // YN - here // YN + XL) % XL
        dy = (named % YN - here % YN + YN) % YN
        places.append((dy * XL + dx) * capacity + slot.astype(jnp.int32))
    return places


def talker_prepare(owners, capacity, values, gain, ids, *outs):
    n = values.shape[0]
    slot = lax.broadcasted_iota(jnp.int32, (owners * capacity, n), 0)
    select = jnp.zeros(slot.shape, F32)
    for place in talker_places(owners, capacity, ids):
        select += jnp.where(slot == place, 1.0, 0.0)
    normed = normalize(values[...], gain[...])
    filled = jnp.dot(select.astype(BF16), normed, preferred_element_type=F32).astype(BF16)
    stay, leave = outs
    for dy in range(YN):
        at = dy * XL * capacity
        stay[dy * capacity : (dy + 1) * capacity, :] = filled[at : at + capacity, :]
        leave[dy * capacity : (dy + 1) * capacity, :] = filled[at + capacity : at + 2 * capacity, :]


def talker_join(capacity, stay, came, *outs):
    for dy, out in enumerate(outs):
        at = slice(dy * capacity, (dy + 1) * capacity)
        out[:capacity, :] = stay[at, :]
        out[capacity:, :] = came[at, :]


def talker_experts(t_gate, t_up, t_down, *refs):
    rows, outs, packed = refs[:YN], refs[YN:-1], refs[-1]
    n = rows[0].shape[0]
    for i, row in enumerate(rows):
        packed[i * n : (i + 1) * n, :] = row[...]
    gate = jnp.dot(packed[...], t_gate[...], preferred_element_type=F32)
    up = jnp.dot(packed[...], t_up[...], preferred_element_type=F32)
    hidden = (gate / (1.0 + jnp.exp(-gate)) * up).astype(BF16)
    result = jnp.dot(hidden, t_down[...], preferred_element_type=F32).astype(BF16)
    for i, out in enumerate(outs):
        out[...] = result[i * n : (i + 1) * n]


def talker_split(capacity, *refs):
    backs, stay, leave = refs[:YN], refs[YN], refs[YN + 1]
    for dy, back in enumerate(backs):
        at = slice(dy * capacity, (dy + 1) * capacity)
        stay[at, :] = back[:capacity, :]
        leave[at, :] = back[capacity:, :]


def talker_finish(owners, capacity, values, ids, gates, state, taps, gain, stayed, came, spoken, audio, kept):
    n = values.shape[0]
    slot = lax.broadcasted_iota(jnp.int32, (owners * capacity, n), 0)
    weight = jnp.zeros(slot.shape, F32)
    for k, place in enumerate(talker_places(owners, capacity, ids)):
        weight += jnp.where(slot == place, gates[k : k + 1, :], 0.0)
    returned = []
    for dy in range(YN):
        at = slice(dy * capacity, (dy + 1) * capacity)
        returned += [stayed[at, :], came[at, :]]
    returned = jnp.concatenate(returned)
    total = jnp.zeros(values.shape, F32)
    for part in three_parts(weight.T):
        total += jnp.dot(part, returned, preferred_element_type=F32)
    fresh = (values[...].astype(F32) + total).astype(BF16)
    spoken[...] = fresh
    newest = fresh.astype(F32)
    frames = state.shape[0]
    mixed = newest * taps[frames : frames + 1, :]
    for j in range(frames):
        mixed += state[j] * taps[j : j + 1, :]
    scale = lax.rsqrt(jnp.mean(mixed * mixed, axis=-1, keepdims=True) + 1e-06)
    audio[...] = (mixed * scale * gain[...]).astype(BF16)
    for j in range(frames - 1):
        kept[j] = state[j + 1]
    kept[frames - 1] = newest


def talker(values, gain, ids, gates, t_gate, t_up, t_down, state, taps, conv_gain):
    n, width = values.shape
    owners = lax.axis_size("sess")
    capacity = min(n, 2 * n * ids.shape[1] // owners)
    half = YN * capacity
    with jax.named_scope("tprep"):
        stay, leave = call(
            functools.partial(talker_prepare, owners, capacity),
            [chip(half, width), chip(half, width)],
            far_args=(values, gain.reshape(1, -1), ids.T),
        )
    came = on_chip(turn(leave, 1, 0, "tx"))
    with jax.named_scope("tjoin"):
        rows = call(functools.partial(talker_join, capacity), [chip(2 * capacity, width)] * YN, stay, came)
    rows = [rows[0]] + [on_chip(turn(rows[dy], 0, dy, f"ty{dy}")) for dy in range(1, YN)]
    with jax.named_scope("texp"):
        outs = call(
            talker_experts,
            [chip(2 * capacity, width)] * YN,
            *rows,
            far_args=(t_gate, t_up, t_down),
            scratch=[pltpu.VMEM((2 * half, width), BF16)],
            limit=10,
        )
    backs = [outs[0]] + [on_chip(turn(outs[dy], 0, -dy, f"tz{dy}")) for dy in range(1, YN)]
    with jax.named_scope("tsplit"):
        stay, leave = call(functools.partial(talker_split, capacity), [chip(half, width)] * 2, *backs)
    came = on_chip(turn(leave, 1, 0, "tw"))
    frames = state.shape[1]
    with jax.named_scope("tfin"):
        spoken, audio, kept = call(
            functools.partial(talker_finish, owners, capacity),
            [shape(n, width), shape(n, width), jax.ShapeDtypeStruct((frames, n, width), F32)],
            stay,
            came,
            far_args=(values, ids.T, gates.T, state.transpose(1, 0, 2), taps, conv_gain.reshape(1, -1)),
        )
    return spoken, audio, kept.transpose(1, 0, 2)


def shards(
    tokens,
    thinker_gain,
    thinker_ids,
    thinker_gates,
    w_gate,
    w_up,
    w_down,
    talker_in,
    talker_gain,
    talker_ids,
    talker_gates,
    t_gate,
    t_up,
    t_down,
    conv_state,
    conv_kernel,
    conv_gain,
):
    thought = thinker(tokens, thinker_gain, thinker_ids, thinker_gates, w_gate[0], w_up[0], w_down[0])
    spoken, audio_frame, new_state = talker(
        talker_in,
        talker_gain,
        talker_ids,
        talker_gates,
        t_gate[0],
        t_up[0],
        t_down[0],
        conv_state,
        conv_kernel,
        conv_gain,
    )
    return (thought, spoken, audio_frame, new_state)


def solution(mesh):
    rows = P(("sess", "exp"), None)
    rows3 = P(("sess", "exp"), None, None)
    placed = (
        rows,
        P(),
        rows,
        rows,
        P("exp", None, None),
        P("exp", None, None),
        P("exp", None, None),
        rows,
        P(),
        rows,
        rows,
        P("sess", None, None),
        P("sess", None, None),
        P("sess", None, None),
        rows3,
        P(),
        P(),
    )
    return jax.shard_map(
        shards,
        mesh=mesh,
        in_specs=placed,
        out_specs=(rows, rows, rows, rows3),
        check_vma=False,
    )
```

```python
import functools

import jax
import jax.numpy as jnp
from jax import lax
from jax.experimental import pallas as pl
from jax.experimental.pallas import tpu as pltpu
from jax.sharding import PartitionSpec as P


XH, ZN, CN = 2, 8, 2
LANES = 128
F32, BF16 = jnp.float32, jnp.bfloat16
VMEM = pl.BlockSpec(memory_space=pltpu.VMEM)
HBM = pl.BlockSpec(memory_space=pltpu.HBM)


def routes(move):
    pairs = []
    for x in range(XH):
        for z in range(ZN):
            for c in range(CN):
                a, b, d = move(x, z, c)
                pairs.append(((x * ZN + z) * CN + c, ((a % XH) * ZN + b % ZN) * CN + d % CN))
    return pairs


RING = routes(lambda x, z, c: (x, z + 1 - 2 * c, c))
CORE = routes(lambda x, z, c: (x, z, c + 1))
CROSS = routes(lambda x, z, c: (x + 1, z, c))


XL, YN = 2, 4


def turns(dx, dy):
    return [(x * YN + y, (x + dx) % XL * YN + (y + dy) % YN) for x in range(XL) for y in range(YN)]


def move(values, route):
    return lax.ppermute(values, "exp", route)


def turn(values, dx, dy):
    return lax.ppermute(values, "sess", turns(dx, dy))


def on_chip(values):
    return pltpu.with_memory_space_constraint(values, pltpu.VMEM)


def off_chip(values):
    return pltpu.with_memory_space_constraint(values, pltpu.HBM)


def call(kernel, out_shape, *args, scratch=(), limit=6, far_args=()):
    fetched = len(far_args)

    def body(*refs):
        sources, refs = refs[:fetched], refs[fetched:]
        if fetched:
            targets, semaphores, refs = refs[-fetched - 1 : -1], refs[-1], refs[: -fetched - 1]
            copies = [
                pltpu.make_async_copy(source, target, semaphores.at[i])
                for i, (source, target) in enumerate(zip(sources, targets))
            ]
            for copy in copies:
                copy.start()
            for copy in copies:
                copy.wait()
            refs = (*targets, *refs)
        kernel(*refs)

    extra = [pltpu.VMEM(arg.shape, arg.dtype) for arg in far_args]
    if fetched:
        extra.append(pltpu.SemaphoreType.DMA((fetched,)))
    return pl.pallas_call(
        body,
        out_shape=out_shape,
        in_specs=[HBM] * fetched + [VMEM] * len(args),
        out_specs=jax.tree.map(lambda _: VMEM, out_shape),
        scratch_shapes=[*scratch, *extra],
        compiler_params=pltpu.CompilerParams(vmem_limit_bytes=limit << 20),
    )(*map(off_chip, far_args), *args)


def shape(rows, columns, dtype=BF16):
    return jax.ShapeDtypeStruct((rows, columns), dtype)


def chip(rows, columns, dtype=BF16):
    return pltpu.VMEM((rows, columns), dtype)


def normalize(values, gain):
    wide = values.astype(F32)
    scale = lax.rsqrt(jnp.mean(wide * wide, axis=-1, keepdims=True) + 1e-06)
    return (wide * scale * gain).astype(BF16)


def three_parts(values):
    high = values.astype(BF16)
    rest = values - high.astype(F32)
    middle = rest.astype(BF16)
    low = (rest - middle.astype(F32)).astype(BF16)
    return high, middle, low


def thinker_prepare(experts, tokens, gain, ids, gates, out):
    width = tokens.shape[1]
    out[:, :width] = normalize(tokens[...], gain[...])
    lane = lax.broadcasted_iota(jnp.int32, (LANES, tokens.shape[0]), 0)
    named = lane % experts
    weight = jnp.zeros(lane.shape, F32)
    for k in range(ids.shape[0]):
        weight += jnp.where(ids[k : k + 1, :] == named, gates[k : k + 1, :], 0.0)
    high, middle, low = (part.astype(F32) for part in three_parts(weight))
    piece = lane // experts
    tags = jnp.where(piece == 0, high, jnp.where(piece == 1, middle, jnp.where(piece == 2, low, 0.0)))
    out[:, width:] = tags.T.astype(BF16)


def pack(first, second, out):
    n = first.shape[0]
    out[:n, :] = first[...]
    out[n:, :] = second[...]


def pack_heads(n, first, second, out):
    out[:n, :] = first[:n, :]
    out[n:, :] = second[:n, :]


def thinker_experts(experts, sizes, gives, fetch, *refs):
    count = len(sizes)
    rows, refs = refs[:count], refs[count:]
    weights, refs = refs[:3], refs[3:]
    packed, hidden, refs = refs[-2], refs[-1], refs[:-2]
    if fetch:
        semaphores, refs = refs[-1], refs[:-1]
        sources, weights, refs = weights, refs[-3:], refs[:-3]
        copies = [pltpu.make_async_copy(sources[i], weights[i], semaphores.at[i]) for i in range(3)]
        for copy in copies:
            copy.start()
    stay, give = refs[: count - gives], refs[count - gives :]
    w_gate, w_up, w_down = weights
    width = w_gate.shape[0]
    expert = lax.axis_index("exp")
    scales, at = [], 0
    for row, n in zip(rows, sizes):
        packed[at : at + n, :] = row[:, :width]
        lane = lax.broadcasted_iota(jnp.int32, (n, LANES), 1)
        chosen = (lane % experts == expert) & (lane < 3 * experts)
        tags = row[:, width:].astype(F32)
        scales.append(jnp.sum(jnp.where(chosen, tags, 0.0), axis=1, keepdims=True))
        at += n
    tile = 256
    if fetch:
        copies[0].wait()
        copies[1].wait()

    def raise_tile(j, carry):
        part = pl.ds(pl.multiple_of(j * tile, tile), tile)
        gate = jnp.dot(packed[...], w_gate[:, part], preferred_element_type=F32)
        up = jnp.dot(packed[...], w_up[:, part], preferred_element_type=F32)
        hidden[:, part] = (gate / (1.0 + jnp.exp(-gate)) * up).astype(BF16)
        return carry

    lax.fori_loop(0, w_gate.shape[1] // tile, raise_tile, 0)
    if fetch:
        copies[2].wait()

    def lower_tile(j, carry):
        part = pl.ds(pl.multiple_of(j * tile, tile), tile)
        result = jnp.dot(hidden[...], w_down[:, part], preferred_element_type=F32).astype(BF16)
        at = 0
        for i, n in enumerate(sizes):
            value = scales[i] * result[at : at + n].astype(F32)
            if i < gives:
                give[0][at : at + n, part] = value.astype(BF16)
            else:
                stay[i - gives][:, part] = value
            at += n
        return carry

    lax.fori_loop(0, width // tile, lower_tile, 0)


def open_chain(stayed, given, out):
    out[...] = (stayed[...] + given[...].astype(F32)).astype(BF16)


def join_chain(n, came, near, far, given, near_out, far_out):
    for half, stayed, out in ((0, near, near_out), (1, far, far_out)):
        base = 2 * n * half
        share = stayed[:n, :] + given[base : base + n, :].astype(F32)
        out[:n, :] = (came[half * n : (half + 1) * n, :].astype(F32) + share).astype(BF16)
        out[n:, :] = (stayed[n:, :] + given[base + n : base + 2 * n, :].astype(F32)).astype(BF16)


def pass_on(base, came, stayed, given, out):
    share = stayed[...] + given[base : base + stayed.shape[0], :].astype(F32)
    out[...] = (came[...].astype(F32) + share).astype(BF16)


def settle(came, own, give, keep):
    n = keep.shape[0]
    give[...] = (came[:n, :].astype(F32) + own[n:, :]).astype(BF16)
    keep[...] = came[n:, :].astype(F32) + own[:n, :]


def close_far(keep, given, out):
    out[...] = (keep[...] + given[...].astype(F32)).astype(BF16)


def close_near(tokens, keep, given, back, out):
    total = keep[...] + given[...].astype(F32) + back[...].astype(F32)
    out[...] = (tokens[...].astype(F32) + total).astype(BF16)


def thinker(tokens, gain, ids, gates, w_gate, w_up, w_down):
    n, width = tokens.shape
    experts = lax.axis_size("exp")
    wide = width + LANES
    rows = call(
        functools.partial(thinker_prepare, experts),
        chip(n, wide),
        far_args=(tokens, gain.reshape(1, -1), ids.T, gates.T),
    )

    def hop(values, route):
        return on_chip(move(values, route))

    beside = hop(rows, CORE)
    across = hop(rows, CROSS)
    near = [call(pack, chip(2 * n, wide), rows, beside)]
    behind = hop(across, CORE)
    far = [call(pack, chip(2 * n, wide), across, behind)]
    for _ in range(1, 4):
        near.append(hop(near[-1], RING))
        far.append(hop(far[-1], RING))
    last = hop(call(functools.partial(pack_heads, n), chip(2 * n, wide), near[3], far[3]), RING)

    weights = [off_chip(w_gate), off_chip(w_up), off_chip(w_down)]
    stayed, given = {}, {}
    plan = [[], [near[1], far[1]], [near[2], far[2]], [near[3], far[3]], [last]]
    for step, mine in enumerate(plan):
        other = [hop(part, CORE) for part in mine]
        fetch, gives = step == 0, len(mine)
        arrays = [*mine, *other] + ([near[0], far[0]] if fetch else [])
        sizes, total = [array.shape[0] for array in arrays], sum(array.shape[0] for array in arrays)
        outs = [chip(size, width, F32) for size in sizes[gives:]]
        if gives:
            outs.append(chip(sum(sizes[:gives]), width))
        scratch = [pltpu.VMEM((total, width), BF16), pltpu.VMEM((total, w_gate.shape[1]), BF16)]
        if fetch:
            outs += [pltpu.VMEM(w.shape, w.dtype) for w in weights]
            scratch.insert(0, pltpu.SemaphoreType.DMA((3,)))
        parts = pl.pallas_call(
            functools.partial(thinker_experts, experts, sizes, gives, fetch),
            out_shape=outs,
            in_specs=[VMEM] * len(arrays) + [HBM if fetch else VMEM] * 3,
            out_specs=[VMEM] * len(outs),
            scratch_shapes=scratch,
            compiler_params=pltpu.CompilerParams(vmem_limit_bytes=16 << 20),
        )(*arrays, *weights)
        if fetch:
            weights = [on_chip(w) for w in parts[-3:]]
        keeps = len(arrays) - gives
        stayed[step] = parts[:keeps]
        if gives:
            given[step] = hop(parts[keeps], CORE)

    first = call(open_chain, chip(2 * n, width), stayed[4][0], given[4])
    first = hop(first, RING)
    near_sum, far_sum = call(
        functools.partial(join_chain, n),
        [chip(2 * n, width)] * 2,
        first,
        stayed[3][0],
        stayed[3][1],
        given[3],
    )
    far_sum, near_sum = hop(far_sum, RING), hop(near_sum, RING)
    for k in (2, 1):
        far_sum = call(functools.partial(pass_on, 2 * n), chip(2 * n, width), far_sum, stayed[k][1], given[k])
        far_sum = hop(far_sum, RING)
        near_sum = call(functools.partial(pass_on, 0), chip(2 * n, width), near_sum, stayed[k][0], given[k])
        near_sum = hop(near_sum, RING)
    give, keep = call(settle, [chip(n, width), chip(n, width, F32)], far_sum, stayed[0][1])
    back = call(close_far, chip(n, width), keep, hop(give, CORE))
    back = hop(back, CROSS)
    give, keep = call(settle, [chip(n, width), chip(n, width, F32)], near_sum, stayed[0][0])
    return call(close_near, shape(n, width), keep, hop(give, CORE), back, far_args=(tokens,))


def talker_places(owners, capacity, ids):
    count, n = ids.shape
    here = lax.axis_index("sess")
    owner = lax.broadcasted_iota(jnp.int32, (owners, n), 0)
    used = jnp.zeros((owners, n), F32)
    for k in range(count):
        used += jnp.where(ids[k : k + 1, :] == owner, 1.0, 0.0)
    row = lax.broadcasted_iota(jnp.int32, (n, n), 0)
    column = lax.broadcasted_iota(jnp.int32, (n, n), 1)
    earlier = jnp.where(row < column, 1.0, 0.0).astype(BF16)
    before = jnp.dot(used.astype(BF16), earlier, preferred_element_type=F32)
    places = []
    for k in range(count):
        named = ids[k : k + 1, :]
        slot = jnp.sum(jnp.where(named == owner, before, 0.0), axis=0, keepdims=True)
        dx = (named // YN - here // YN + XL) % XL
        dy = (named % YN - here % YN + YN) % YN
        places.append((dy * XL + dx) * capacity + slot.astype(jnp.int32))
    return places


def talker_prepare(owners, capacity, values, gain, ids, *outs):
    n = values.shape[0]
    slot = lax.broadcasted_iota(jnp.int32, (owners * capacity, n), 0)
    select = jnp.zeros(slot.shape, F32)
    for place in talker_places(owners, capacity, ids):
        select += jnp.where(slot == place, 1.0, 0.0)
    normed = normalize(values[...], gain[...])
    filled = jnp.dot(select.astype(BF16), normed, preferred_element_type=F32).astype(BF16)
    stay, leave = outs
    for dy in range(YN):
        at = dy * XL * capacity
        stay[dy * capacity : (dy + 1) * capacity, :] = filled[at : at + capacity, :]
        leave[dy * capacity : (dy + 1) * capacity, :] = filled[at + capacity : at + 2 * capacity, :]


def talker_join(capacity, stay, came, *outs):
    for dy, out in enumerate(outs):
        at = slice(dy * capacity, (dy + 1) * capacity)
        out[:capacity, :] = stay[at, :]
        out[capacity:, :] = came[at, :]


def talker_experts(t_gate, t_up, t_down, *refs):
    rows, outs, packed = refs[:YN], refs[YN:-1], refs[-1]
    n = rows[0].shape[0]
    for i, row in enumerate(rows):
        packed[i * n : (i + 1) * n, :] = row[...]
    gate = jnp.dot(packed[...], t_gate[...], preferred_element_type=F32)
    up = jnp.dot(packed[...], t_up[...], preferred_element_type=F32)
    hidden = (gate / (1.0 + jnp.exp(-gate)) * up).astype(BF16)
    result = jnp.dot(hidden, t_down[...], preferred_element_type=F32).astype(BF16)
    for i, out in enumerate(outs):
        out[...] = result[i * n : (i + 1) * n]


def talker_split(capacity, *refs):
    backs, stay, leave = refs[:YN], refs[YN], refs[YN + 1]
    for dy, back in enumerate(backs):
        at = slice(dy * capacity, (dy + 1) * capacity)
        stay[at, :] = back[:capacity, :]
        leave[at, :] = back[capacity:, :]


def talker_finish(owners, capacity, values, ids, gates, state, taps, gain, stayed, came, spoken, audio, kept):
    n = values.shape[0]
    slot = lax.broadcasted_iota(jnp.int32, (owners * capacity, n), 0)
    weight = jnp.zeros(slot.shape, F32)
    for k, place in enumerate(talker_places(owners, capacity, ids)):
        weight += jnp.where(slot == place, gates[k : k + 1, :], 0.0)
    returned = []
    for dy in range(YN):
        at = slice(dy * capacity, (dy + 1) * capacity)
        returned += [stayed[at, :], came[at, :]]
    returned = jnp.concatenate(returned)
    total = jnp.zeros(values.shape, F32)
    for part in three_parts(weight.T):
        total += jnp.dot(part, returned, preferred_element_type=F32)
    fresh = (values[...].astype(F32) + total).astype(BF16)
    spoken[...] = fresh
    newest = fresh.astype(F32)
    frames = state.shape[0]
    mixed = newest * taps[frames : frames + 1, :]
    for j in range(frames):
        mixed += state[j] * taps[j : j + 1, :]
    scale = lax.rsqrt(jnp.mean(mixed * mixed, axis=-1, keepdims=True) + 1e-06)
    audio[...] = (mixed * scale * gain[...]).astype(BF16)
    for j in range(frames - 1):
        kept[j] = state[j + 1]
    kept[frames - 1] = newest


def talker(values, gain, ids, gates, t_gate, t_up, t_down, state, taps, conv_gain):
    n, width = values.shape
    owners = lax.axis_size("sess")
    capacity = min(n, 2 * n * ids.shape[1] // owners)
    half = YN * capacity
    stay, leave = call(
        functools.partial(talker_prepare, owners, capacity),
        [chip(half, width), chip(half, width)],
        far_args=(values, gain.reshape(1, -1), ids.T),
    )
    came = on_chip(turn(leave, 1, 0))
    rows = call(functools.partial(talker_join, capacity), [chip(2 * capacity, width)] * YN, stay, came)
    rows = [rows[0]] + [on_chip(turn(rows[dy], 0, dy)) for dy in range(1, YN)]
    outs = call(
        talker_experts,
        [chip(2 * capacity, width)] * YN,
        *rows,
        far_args=(t_gate, t_up, t_down),
        scratch=[pltpu.VMEM((2 * half, width), BF16)],
        limit=10,
    )
    backs = [outs[0]] + [on_chip(turn(outs[dy], 0, -dy)) for dy in range(1, YN)]
    stay, leave = call(functools.partial(talker_split, capacity), [chip(half, width)] * 2, *backs)
    came = on_chip(turn(leave, 1, 0))
    frames = state.shape[1]
    spoken, audio, kept = call(
        functools.partial(talker_finish, owners, capacity),
        [shape(n, width), shape(n, width), jax.ShapeDtypeStruct((frames, n, width), F32)],
        stay,
        came,
        far_args=(values, ids.T, gates.T, state.transpose(1, 0, 2), taps, conv_gain.reshape(1, -1)),
    )
    return spoken, audio, kept.transpose(1, 0, 2)


def layers(
    tokens,
    thinker_gain,
    thinker_ids,
    thinker_gates,
    w_gate,
    w_up,
    w_down,
    talker_in,
    talker_gain,
    talker_ids,
    talker_gates,
    t_gate,
    t_up,
    t_down,
    conv_state,
    conv_kernel,
    conv_gain,
):
    thought = thinker(tokens, thinker_gain, thinker_ids, thinker_gates, w_gate[0], w_up[0], w_down[0])
    spoken, audio_frame, new_state = talker(
        talker_in,
        talker_gain,
        talker_ids,
        talker_gates,
        t_gate[0],
        t_up[0],
        t_down[0],
        conv_state,
        conv_kernel,
        conv_gain,
    )
    return (thought, spoken, audio_frame, new_state)


def solution(mesh):
    rows = P(("sess", "exp"), None)
    rows3 = P(("sess", "exp"), None, None)
    placed = (
        rows,
        P(),
        rows,
        rows,
        P("exp", None, None),
        P("exp", None, None),
        P("exp", None, None),
        rows,
        P(),
        rows,
        rows,
        P("sess", None, None),
        P("sess", None, None),
        P("sess", None, None),
        rows3,
        P(),
        P(),
    )
    return jax.shard_map(
        layers,
        mesh=mesh,
        in_specs=placed,
        out_specs=(rows, rows, rows, rows3),
        check_vma=False,
    )
```
